32 devices in a mesh: dp: 16 (over z, x, core), expert: 2 (over y).
Axes of the slice: x: 2, y: 2, z: 4, core: 2. Of those that a mesh axis runs over, the one named last changes fastest.
Arguments:
- hidden: bfloat16 [1024, 8192], P(('dp', 'expert')), may hold values from -6 to 6
- out_grad: bfloat16 [1024, 6144], P(('dp', 'expert')), may hold values from -6 to 6
- counts: int32 [32, 2], P(('dp', 'expert')), may hold values from 0 to 20, as said below
- route_index: int32 [32, 32], P(('dp', 'expert')), may hold values from 0 to 31, each once within a row
- keep: int32 [16], replicated, may hold values 0 or 1
Outputs:
- grad_blocks: float32 [2, 16, 2048, 1536], P('expert', 'dp')
- block_scales: float32 [2, 16, 2048, 12], P('expert', 'dp')
The draws below stay inside these ranges and needn't reach their ends.
Inputs may be any that keep to these rules, and one draw needn't show every extreme that they name: Each row of counts sums to 32; for every index of dp, one expert receives exactly 20 rows from each of the 2 devices of that index.
All inputs are finite; a program needn't handle non-finite values. Where the reference program divides by a largest or mean magnitude, that divisor is 1e-20 or more.
Results may differ from the reference program's by a relative error of at most 0.0003.
Values may be sent and summed in bfloat16 or wider, within the bound.
A program may use at most 128 MiB of HBM per device.

```python
import jax
import jax.numpy as jnp
from jax import lax

D = 6144
HW = 8192
TOK_DEV = 32
CAP = 20
Q = 4
TOKENS = 1024
N_DP = 16
N_EXPERT = 2


def draw_counts(key, part):
    experts = N_EXPERT
    devices = N_DP * N_EXPERT
    key_hot = jax.random.fold_in(key, 11)
    key_weight = jax.random.fold_in(key, 23)
    hot = jax.random.randint(key_hot, (N_DP,), 0, experts)
    hot_dev = jnp.repeat(hot, experts)
    others = experts - 1
    rest = TOK_DEV - CAP
    weights = jax.random.randint(key_weight, (devices, others), 1, 3)
    total = jnp.sum(weights, axis=1, keepdims=True)
    base = rest * weights // total
    remain = rest - jnp.sum(base, axis=1, keepdims=True)
    extra = (jnp.arange(others)[None, :] < remain).astype(jnp.int32)
    split = base + extra
    column = jnp.arange(experts)[None, :]
    offset = (column - hot_dev[:, None] - 1) % experts
    offset = jnp.minimum(offset, others - 1)
    values = jnp.take_along_axis(split, offset, axis=1)
    result = jnp.where(column == hot_dev[:, None], CAP, values)
    return result.astype(jnp.int32)


def place_ends(array, stream_key, least, largest):
    index_at = [jax.random.randint(jax.random.fold_in(stream_key, axis), (), 0, length) for axis, length in enumerate(array.shape)]
    widest = array.shape.index(max(array.shape))
    beside = index_at[:widest] + [(index_at[widest] + 1) % array.shape[widest]] + index_at[widest + 1:]
    return array.at[tuple(index_at)].set(least).at[tuple(beside)].set(largest)


def block_levels(key, dims, shards, low, top_value):
    factor_of = 1.0
    for dim, blocks in shards:
        heights = jax.random.uniform(jax.random.fold_in(jax.random.fold_in(key, 6), dim), (blocks,), jnp.float32, low / len(shards), top_value / len(shards))
        factor_of = factor_of * jnp.repeat(jnp.exp(heights), dims[dim] // blocks).reshape((-1,) + (1,) * (len(dims) - 1 - dim))
    return factor_of


def normal_values(key, shape, width, limit, cuts=(), kind=jnp.bfloat16):
    array = width * jax.random.normal(key, shape, jnp.float32)
    if cuts:
        array = array * block_levels(key, shape, cuts, -0.22, 0.18)
    return jnp.clip(array, -limit, limit).astype(kind)


def setup_inputs(seed: int = 0) -> dict:
    arg_keys = jax.random.split(jax.random.key(seed), 6)
    return {
        "hidden": normal_values(arg_keys[0], (TOKENS, HW), 1.0, 6.0, ((0, 32),)),
        "out_grad": normal_values(arg_keys[1], (TOKENS, D), 1.0, 6.0, ((0, 32),)),
        "counts": draw_counts(jax.random.fold_in(arg_keys[5], 71), 0),
        "route_index": jax.vmap(lambda own: jax.random.permutation(own, TOK_DEV))(jax.random.split(arg_keys[3], (N_DP * N_EXPERT))).reshape((N_DP * N_EXPERT, TOK_DEV)).astype(jnp.int32),
        "keep": place_ends((jax.random.randint(arg_keys[4], (N_DP,), 0, 4) < 3).astype(jnp.int32), jax.random.fold_in(arg_keys[4], 1), 0, 1),
    }


def expert_rows(rows_dev, counts_dev, perm_dev, expert_id):
    offsets = jnp.cumsum(counts_dev) - counts_dev
    start = offsets[expert_id]
    count = counts_dev[expert_id]
    slots = jnp.arange(CAP, dtype=jnp.int32)
    position = jnp.minimum(start + slots, TOK_DEV - 1).astype(jnp.int32)
    local = perm_dev[position]
    picked = rows_dev[local]
    return jnp.where((slots < count)[:, None], picked, jnp.zeros_like(picked))


def reference(hidden, out_grad, counts, route_index, keep):
    ndev = N_DP * N_EXPERT
    hid_dev = hidden.reshape(ndev, TOK_DEV, HW)
    grad_dev = out_grad.reshape(ndev, TOK_DEV, D)
    keep_dev = jnp.repeat(keep, N_EXPERT)
    grad_dev = jnp.where((keep_dev > 0)[:, None, None], grad_dev, jnp.zeros_like(grad_dev))
    kept = jnp.sum(keep).astype(jnp.float32)
    factor = jnp.float32(N_DP) / jnp.maximum(kept, jnp.float32(1.0))
    tile_rows = HW // Q
    tile_cols = D // Q

    def one_expert(expert_id):
        gather_rows = jax.vmap(expert_rows, in_axes=(0, 0, 0, None))
        rows_h = gather_rows(hid_dev, counts, route_index, expert_id).reshape(ndev * CAP, HW)
        rows_g = gather_rows(grad_dev, counts, route_index, expert_id).reshape(ndev * CAP, D)
        grad = lax.dot_general(rows_h, rows_g, (((0,), (0,)), ((), ())), preferred_element_type=jnp.float32)
        grad = grad * factor
        blocked = grad.reshape(HW, D // 128, 128)
        scales = jnp.max(jnp.abs(blocked), axis=-1)
        normed = (blocked / (scales[..., None] + 1e-6)).reshape(HW, D)
        tiles = normed.reshape(Q, tile_rows, Q, tile_cols).transpose(0, 2, 1, 3).reshape(N_DP, tile_rows, tile_cols)
        scale_tiles = scales.reshape(Q, tile_rows, Q, tile_cols // 128).transpose(0, 2, 1, 3).reshape(N_DP, tile_rows, tile_cols // 128)
        return tiles, scale_tiles

    return lax.map(one_expert, jnp.arange(N_EXPERT, dtype=jnp.int32))
```

```python
import functools
import math

import jax
import jax.numpy as jnp
from jax import lax
from jax.experimental import pallas as pl
from jax.experimental.pallas import tpu as pltpu
from jax.sharding import PartitionSpec as P

MESH = pl.DeviceIdType.MESH
LANES = 128
SUB = 16


def swapped(block, axis, bit):
    count = lax.axis_size(axis)
    route = []
    for low in range(count):
        high = low | 1 << bit
        if high != low and high < count:
            route += [(low, high), (high, low)]
    return lax.ppermute(block, axis, route)


def build_slots(rows_dev, counts_dev, perm_dev, capacity):
    offsets = jnp.cumsum(counts_dev) - counts_dev
    slots = jnp.arange(capacity, dtype=jnp.int32)
    position = offsets[:, None] + slots[None, :]
    position = jnp.minimum(position, rows_dev.shape[0] - 1)
    live = slots[None, :] < counts_dev[:, None]
    local = perm_dev[position]
    picked = rows_dev[local]
    return jnp.where(live[:, :, None], picked, jnp.zeros_like(picked))


def join_pair(mine, partner, replica, bit):
    lower = replica >> bit & 1 == 0
    first = jnp.concatenate([mine, partner], axis=1)
    second = jnp.concatenate([partner, mine], axis=1)
    return jnp.where(lower, first, second)


def gather_general(hidden, out_grad, counts, route_index, keep, capacity):
    experts = lax.axis_size("expert")
    replicas = lax.axis_size("dp")
    side = math.isqrt(replicas)
    levels = side.bit_length() - 1
    replica = lax.axis_index("dp")
    hidden_units = hidden.shape[1]
    width = out_grad.shape[1]
    grad_rows = jnp.where(keep[replica] > 0, out_grad, jnp.zeros_like(out_grad))
    send_h = build_slots(hidden, counts[0], route_index[0], capacity)
    send_g = build_slots(grad_rows, counts[0], route_index[0], capacity)
    recv_h = lax.all_to_all(send_h, "expert", split_axis=0, concat_axis=0, tiled=True)
    recv_g = lax.all_to_all(send_g, "expert", split_axis=0, concat_axis=0, tiled=True)
    slot_count = experts * capacity
    tile_rows = hidden_units // side
    tile_cols = width // side
    sub_rows = slot_count // side
    piece_h = (
        recv_h.reshape(side, sub_rows, side, tile_rows)
        .transpose(2, 0, 1, 3)
        .reshape(replicas, sub_rows, tile_rows)
    )
    piece_g = (
        recv_g.reshape(side, sub_rows, side, tile_cols)
        .transpose(0, 2, 1, 3)
        .reshape(replicas, sub_rows, tile_cols)
    )
    all_h = lax.all_to_all(piece_h, "dp", split_axis=0, concat_axis=0, tiled=True)
    all_g = lax.all_to_all(piece_g, "dp", split_axis=0, concat_axis=0, tiled=True)
    for bit in range(levels):
        all_h = join_pair(all_h, swapped(all_h, "dp", bit), replica, bit)
    for bit in range(levels, 2 * levels):
        all_g = join_pair(all_g, swapped(all_g, "dp", bit), replica, bit)
    return [(all_h.reshape(-1, tile_rows), all_g.reshape(-1, tile_cols))]


def slots_kernel(side, big, rest, counts, keep, route, hidden, grad, h_o, h_c, g_o, g_c):
    me = lax.axis_index("expert")
    rows = hidden.shape[0]
    total = 2 * big + 4 * rest
    row = lax.broadcasted_iota(jnp.int32, (total, rows), 0)
    pos = lax.broadcasted_iota(jnp.int32, (total, rows), 1)
    tail = row >= 2 * big
    in_tail = row - 2 * big
    other = jnp.logical_or(
        in_tail >= 2 * rest, jnp.logical_and(row >= big, jnp.logical_not(tail))
    )
    tail_row = jnp.where(in_tail >= 2 * rest, in_tail - 2 * rest, in_tail) - me * rest
    slot = jnp.where(tail, big + tail_row, jnp.where(row >= big, row - big, row))
    valid = jnp.logical_or(
        jnp.logical_not(tail), jnp.logical_and(tail_row >= 0, tail_row < rest)
    )
    first, second = counts[0, 0], counts[0, 1]
    expert = jnp.where(other, 1 - me, me)
    start = jnp.where(expert == 0, 0, first)
    count = jnp.where(expert == 0, first, second)
    take = jnp.logical_and(valid, jnp.logical_and(slot < count, pos == start + slot))
    take = jnp.where(take, 1.0, 0.0).astype(jnp.bfloat16)
    local = lax.broadcasted_iota(jnp.int32, (rows, rows), 0)
    perm = jnp.where(local == route[...], 1.0, 0.0).astype(jnp.bfloat16)
    pick = lax.dot_general(
        take, perm, (((1,), (1,)), ((), ())), preferred_element_type=jnp.float32
    )
    kept = keep[lax.axis_index("dp")] > 0
    pick_h = pick.astype(jnp.bfloat16)
    pick_g = jnp.where(kept, pick, 0.0).astype(jnp.bfloat16)
    for pick_x, src, o_ref, c_ref in ((pick_h, hidden, h_o, h_c), (pick_g, grad, g_o, g_c)):
        cols = o_ref.shape[3]
        for part in range(side):
            got = jnp.dot(
                pick_x,
                src[:, part * cols : (part + 1) * cols],
                preferred_element_type=jnp.float32,
            ).astype(jnp.bfloat16)
            for k in range(2):
                o_ref[k, part] = got[k * big : (k + 1) * big]
                low = 2 * big + 2 * rest * k
                c_ref[k, part] = got[low : low + 2 * rest]


def spread_kernel(
    n, h_o, h_c, g_o, g_c, hh, hc, gg, gc, ph, phc, pg, pgc, sh, sg,
    send_sem, h_sem, g_sem, y_sem, own_sem,
):
    here = lax.axis_index("dp")
    y = lax.axis_index("expert")
    z, q = here // n, here % n
    zs = [(z + d) % n for d in range(n)]
    qs = [(q + d) % n for d in range(n)]

    barrier = pltpu.get_barrier_semaphore()
    peers = [(here, 1 - y)]
    peers += [(zs[d] * n + q, y) for d in range(1, n)]
    peers += [(z * n + qs[d], y) for d in range(1, n)]
    for peer in peers:
        pl.semaphore_signal(barrier, inc=1, device_id=peer, device_id_type=MESH)
    pl.semaphore_wait(barrier, len(peers))

    ends = []

    def send(src, dst, sem, peer, when=None):
        copy = pltpu.make_async_remote_copy(
            src_ref=src,
            dst_ref=dst,
            send_sem=send_sem.at[len(ends)],
            recv_sem=sem,
            device_id=peer,
            device_id_type=MESH,
        )
        ends.append((copy, when))
        if when is None:
            copy.start()
        else:
            pl.when(when)(copy.start)

    def landed(view, sem):
        pltpu.make_async_copy(view, view, sem).wait()

    h_at = lambda i, b: hh.at[i, b] if b < 2 else hc.at[i]
    g_at = lambda i, b: gg.at[i, b] if b < 2 else gc.at[i]
    h_from = lambda b, i: (h_o.at[0, i], ph.at[i], sh.at[i])[b]
    g_from = lambda b, i: (g_o.at[0, i], pg.at[i], sg.at[i])[b]
    hs = lambda i, b: h_sem.at[i * 3 + b]
    gs = lambda i, b: g_sem.at[i * 3 + b]
    own = []

    def keep_own(src, dst):
        copy = pltpu.make_async_copy(src, dst, own_sem.at[len(own)])
        copy.start()
        own.append(copy)

    def fan_h(src, i, b):
        for d in range(1, n):
            send(src, h_at(i, b), hs(i, b), (z * n + qs[d], y))

    def up_g(src, i, b, ok=None):
        when = z + 1 < n
        when = when if ok is None else jnp.logical_and(when, ok)
        send(src, g_at(i, b), gs(i, b), (jnp.minimum(z + 1, n - 1) * n + q, y), when)

    def down_g(src, i, b, ok=None):
        when = z >= 1
        when = when if ok is None else jnp.logical_and(when, ok)
        send(src, g_at(i, b), gs(i, b), (jnp.maximum(z - 1, 0) * n + q, y), when)

    def start_block(b):
        for d in range(1, n):
            send(g_from(b, qs[d]), g_at(here, b), gs(here, b), (z * n + qs[d], y))
        for d in range(1, n):
            send(h_from(b, zs[d]), h_at(here, b), hs(here, b), (zs[d] * n + q, y))
        fan_h(h_from(b, z), here, b)
        up_g(g_from(b, q), here, b)
        down_g(g_from(b, q), here, b)
        keep_own(h_from(b, z), h_at(here, b))
        keep_own(g_from(b, q), g_at(here, b))

    def plane_g(b):
        for d in range(1, n):
            i = z * n + qs[d]
            landed(g_at(i, b), gs(i, b))
            up_g(g_at(i, b), i, b)
            down_g(g_at(i, b), i, b)

    def arrive_h(b):
        for d in range(1, n):
            i = zs[d] * n + q
            landed(h_at(i, b), hs(i, b))
            fan_h(h_at(i, b), i, b)

    def forward_g(b, d):
        for k in range(n):
            low = jnp.maximum(z - d, 0) * n + k
            high = jnp.minimum(z + d, n - 1) * n + k

            @pl.when(z - d >= 0)
            def _():
                landed(g_at(low, b), gs(low, b))

            if d < n - 1:
                up_g(g_at(low, b), low, b, z - d >= 0)

            @pl.when(z + d < n)
            def _():
                landed(g_at(high, b), gs(high, b))

            if d < n - 1:
                down_g(g_at(high, b), high, b, z + d < n)

    def partner(b):
        if b == 1:
            for i in range(n):
                landed(ph.at[i], y_sem.at[i])
                landed(pg.at[i], y_sem.at[n + i])
        else:
            landed(phc, y_sem.at[2 * n])
            landed(pgc, y_sem.at[2 * n + 1])
            sh[...] = h_c[0] + phc[...]
            sg[...] = g_c[0] + pgc[...]

    across = (here, 1 - y)
    for i in range(n):
        send(g_o.at[1, i], pg.at[i], y_sem.at[n + i], across)
        send(h_o.at[1, i], ph.at[i], y_sem.at[i], across)
    send(h_c.at[1], phc, y_sem.at[2 * n], across)
    send(g_c.at[1], pgc, y_sem.at[2 * n + 1], across)
    start_block(0)
    plane_g(0)
    partner(1)
    start_block(1)
    arrive_h(0)
    plane_g(1)
    forward_g(0, 1)
    partner(2)
    arrive_h(1)
    start_block(2)
    forward_g(1, 1)
    forward_g(0, 2)
    plane_g(2)
    arrive_h(2)
    for d in range(1, n):
        for b in range(3):
            if (b, d) not in ((0, 1), (1, 1), (0, 2)):
                forward_g(b, d)
    for b in range(3):
        for d in range(1, n):
            for zz in range(n):
                i = zz * n + qs[d]
                landed(h_at(i, b), hs(i, b))
    for copy in own:
        copy.wait()
    for copy, when in ends:
        if when is None:
            copy.wait_send()
        else:
            pl.when(when)(copy.wait_send)


def n_sends(n):
    block = 2 * (n - 1) + (n - 1) + 2
    plane = 2 * (n - 1)
    arrive = (n - 1) * (n - 1)
    forward = (n - 2) * n * 2
    return 2 * n + 2 + 3 * (block + plane + arrive + forward)


def gather_pairs(hidden, out_grad, counts, route_index, keep, capacity):
    replicas = lax.axis_size("dp")
    n = math.isqrt(replicas)
    hcols, gcols = hidden.shape[1] // n, out_grad.shape[1] // n
    big = capacity // SUB * SUB
    rest = capacity - big
    kind = jnp.bfloat16
    vmem = pl.BlockSpec(memory_space=pltpu.VMEM)
    smem = pl.BlockSpec(memory_space=pltpu.SMEM)
    made = pl.pallas_call(
        functools.partial(slots_kernel, n, big, rest),
        out_shape=[
            jax.ShapeDtypeStruct((2, n, big, hcols), kind),
            jax.ShapeDtypeStruct((2, n, 2 * rest, hcols), kind),
            jax.ShapeDtypeStruct((2, n, big, gcols), kind),
            jax.ShapeDtypeStruct((2, n, 2 * rest, gcols), kind),
        ],
        in_specs=[smem, smem, vmem, vmem, vmem],
        out_specs=[vmem] * 4,
        name="slots",
    )(counts, keep, route_index, hidden, out_grad)
    hh, hc, gg, gc = pl.pallas_call(
        functools.partial(spread_kernel, n),
        out_shape=[
            jax.ShapeDtypeStruct((replicas, 2, big, hcols), kind),
            jax.ShapeDtypeStruct((replicas, 2 * rest, hcols), kind),
            jax.ShapeDtypeStruct((replicas, 2, big, gcols), kind),
            jax.ShapeDtypeStruct((replicas, 2 * rest, gcols), kind),
        ],
        in_specs=[vmem] * 4,
        out_specs=[vmem] * 4,
        scratch_shapes=[
            pltpu.VMEM((n, big, hcols), kind),
            pltpu.VMEM((n, 2 * rest, hcols), kind),
            pltpu.VMEM((n, big, gcols), kind),
            pltpu.VMEM((n, 2 * rest, gcols), kind),
            pltpu.VMEM((n, 2 * rest, hcols), kind),
            pltpu.VMEM((n, 2 * rest, gcols), kind),
            pltpu.SemaphoreType.DMA((n_sends(n),)),
            pltpu.SemaphoreType.DMA((replicas * 3,)),
            pltpu.SemaphoreType.DMA((replicas * 3,)),
            pltpu.SemaphoreType.DMA((2 * n + 2,)),
            pltpu.SemaphoreType.DMA((6,)),
        ],
        compiler_params=pltpu.CompilerParams(collective_id=0, has_side_effects=True),
        name="spread",
    )(*made)
    return [
        (hh.reshape(-1, hcols), gg.reshape(-1, gcols)),
        (hc.reshape(-1, hcols), gc.reshape(-1, gcols)),
    ]


def tile_kernel(pairs, keep, *refs):
    out, scales = refs[2 * pairs :]
    replicas = keep.shape[0]
    kept = keep[0]
    for i in range(1, replicas):
        kept = kept + keep[i]
    factor = jnp.float32(replicas) / jnp.maximum(
        jnp.full((1, LANES), kept, jnp.int32).astype(jnp.float32), 1.0
    )
    total = None
    for i in range(pairs):
        term = lax.dot_general(
            refs[2 * i][...],
            refs[2 * i + 1][...],
            (((0,), (0,)), ((), ())),
            preferred_element_type=jnp.float32,
        )
        total = term if total is None else total + term
    tops = []
    for b in range(out.shape[1] // LANES):
        block = total[:, b * LANES : (b + 1) * LANES] * factor
        top = jnp.max(jnp.abs(block), axis=1, keepdims=True)
        out[:, b * LANES : (b + 1) * LANES] = block * (1.0 / (top + 1e-6))
        tops.append(top)
    scales[...] = jnp.concatenate(tops, axis=1)


def tile_grad(pairs, keep):
    rows, cols = pairs[0][0].shape[1], pairs[0][1].shape[1]
    step = min(rows, 256)
    args, specs = [], []
    for h, g in pairs:
        args += [h, g]
        specs.append(pl.BlockSpec((h.shape[0], step), lambda i: (0, i)))
        specs.append(pl.BlockSpec((g.shape[0], cols), lambda i: (0, 0)))
    return pl.pallas_call(
        functools.partial(tile_kernel, len(pairs)),
        grid=(rows // step,),
        out_shape=[
            jax.ShapeDtypeStruct((rows, cols), jnp.float32),
            jax.ShapeDtypeStruct((rows, cols // LANES), jnp.float32),
        ],
        in_specs=[pl.BlockSpec(memory_space=pltpu.SMEM)] + specs,
        out_specs=[
            pl.BlockSpec((step, cols), lambda i: (i, 0)),
            pl.BlockSpec((step, cols // LANES), lambda i: (i, 0)),
        ],
        name="tile_grad",
    )(keep, *args)


def on_device(hidden, out_grad, counts, route_index, keep):
    experts = lax.axis_size("expert")
    tok_rows = hidden.shape[0]
    capacity = max(tok_rows // 4, tok_rows // experts + 4)
    rest = capacity % SUB
    paired = experts == 2 and capacity == SUB + rest and 2 * rest == SUB // 2
    gather = gather_pairs if paired else gather_general
    pairs = gather(hidden, out_grad, counts, route_index, keep, capacity)
    normed, scales = tile_grad(pairs, keep)
    return (normed[None, None], scales[None, None])


def solution(mesh):
    placed = (
        P(("dp", "expert"), None),
        P(("dp", "expert"), None),
        P(("dp", "expert"), None),
        P(("dp", "expert"), None),
        P(),
    )
    return jax.shard_map(
        on_device,
        mesh=mesh,
        in_specs=placed,
        out_specs=(P("expert", "dp", None, None), P("expert", "dp", None, None)),
        check_vma=False,
    )
```

```python
import functools
import math

import jax
import jax.numpy as jnp
from jax import lax
from jax.experimental import pallas as pl
from jax.experimental.pallas import tpu as pltpu
from jax.sharding import PartitionSpec as P

MESH = pl.DeviceIdType.MESH
LANES = 128
SUB = 16


def swapped(block, axis, bit):
    count = lax.axis_size(axis)
    route = []
    for low in range(count):
        high = low | 1 << bit
        if high != low and high < count:
            route += [(low, high), (high, low)]
    return lax.ppermute(block, axis, route)


def build_slots(rows_dev, counts_dev, perm_dev, capacity):
    offsets = jnp.cumsum(counts_dev) - counts_dev
    slots = jnp.arange(capacity, dtype=jnp.int32)
    position = offsets[:, None] + slots[None, :]
    position = jnp.minimum(position, rows_dev.shape[0] - 1)
    live = slots[None, :] < counts_dev[:, None]
    local = perm_dev[position]
    picked = rows_dev[local]
    return jnp.where(live[:, :, None], picked, jnp.zeros_like(picked))


def join_pair(mine, partner, replica, bit):
    lower = replica >> bit & 1 == 0
    first = jnp.concatenate([mine, partner], axis=1)
    second = jnp.concatenate([partner, mine], axis=1)
    return jnp.where(lower, first, second)


def gather_general(hidden, out_grad, counts, route_index, keep, capacity):
    experts = lax.axis_size("expert")
    replicas = lax.axis_size("dp")
    side = math.isqrt(replicas)
    levels = side.bit_length() - 1
    replica = lax.axis_index("dp")
    hidden_units = hidden.shape[1]
    width = out_grad.shape[1]
    grad_rows = jnp.where(keep[replica] > 0, out_grad, jnp.zeros_like(out_grad))
    send_h = build_slots(hidden, counts[0], route_index[0], capacity)
    send_g = build_slots(grad_rows, counts[0], route_index[0], capacity)
    recv_h = lax.all_to_all(send_h, "expert", split_axis=0, concat_axis=0, tiled=True)
    recv_g = lax.all_to_all(send_g, "expert", split_axis=0, concat_axis=0, tiled=True)
    slot_count = experts * capacity
    tile_rows = hidden_units // side
    tile_cols = width // side
    sub_rows = slot_count // side
    piece_h = (
        recv_h.reshape(side, sub_rows, side, tile_rows)
        .transpose(2, 0, 1, 3)
        .reshape(replicas, sub_rows, tile_rows)
    )
    piece_g = (
        recv_g.reshape(side, sub_rows, side, tile_cols)
        .transpose(0, 2, 1, 3)
        .reshape(replicas, sub_rows, tile_cols)
    )
    all_h = lax.all_to_all(piece_h, "dp", split_axis=0, concat_axis=0, tiled=True)
    all_g = lax.all_to_all(piece_g, "dp", split_axis=0, concat_axis=0, tiled=True)
    for bit in range(levels):
        all_h = join_pair(all_h, swapped(all_h, "dp", bit), replica, bit)
    for bit in range(levels, 2 * levels):
        all_g = join_pair(all_g, swapped(all_g, "dp", bit), replica, bit)
    return [(all_h.reshape(-1, tile_rows), all_g.reshape(-1, tile_cols))]


def slots_kernel(side, big, rest, counts, keep, route, hidden, grad, h_o, h_c, g_o, g_c):
    me = lax.axis_index("expert")
    rows = hidden.shape[0]
    total = 2 * big + 4 * rest
    row = lax.broadcasted_iota(jnp.int32, (total, rows), 0)
    pos = lax.broadcasted_iota(jnp.int32, (total, rows), 1)
    tail = row >= 2 * big
    in_tail = row - 2 * big
    other = jnp.logical_or(
        in_tail >= 2 * rest, jnp.logical_and(row >= big, jnp.logical_not(tail))
    )
    tail_row = jnp.where(in_tail >= 2 * rest, in_tail - 2 * rest, in_tail) - me * rest
    slot = jnp.where(tail, big + tail_row, jnp.where(row >= big, row - big, row))
    valid = jnp.logical_or(
        jnp.logical_not(tail), jnp.logical_and(tail_row >= 0, tail_row < rest)
    )
    first, second = counts[0, 0], counts[0, 1]
    expert = jnp.where(other, 1 - me, me)
    start = jnp.where(expert == 0, 0, first)
    count = jnp.where(expert == 0, first, second)
    take = jnp.logical_and(valid, jnp.logical_and(slot < count, pos == start + slot))
    take = jnp.where(take, 1.0, 0.0).astype(jnp.bfloat16)
    local = lax.broadcasted_iota(jnp.int32, (rows, rows), 0)
    perm = jnp.where(local == route[...], 1.0, 0.0).astype(jnp.bfloat16)
    pick = lax.dot_general(
        take, perm, (((1,), (1,)), ((), ())), preferred_element_type=jnp.float32
    )
    kept = keep[lax.axis_index("dp")] > 0
    pick_h = pick.astype(jnp.bfloat16)
    pick_g = jnp.where(kept, pick, 0.0).astype(jnp.bfloat16)
    for pick_x, src, o_ref, c_ref in ((pick_h, hidden, h_o, h_c), (pick_g, grad, g_o, g_c)):
        cols = o_ref.shape[3]
        for part in range(side):
            got = jnp.dot(
                pick_x,
                src[:, part * cols : (part + 1) * cols],
                preferred_element_type=jnp.float32,
            ).astype(jnp.bfloat16)
            for k in range(2):
                o_ref[k, part] = got[k * big : (k + 1) * big]
                low = 2 * big + 2 * rest * k
                c_ref[k, part] = got[low : low + 2 * rest]


def spread_kernel(
    n, h_o, h_c, g_o, g_c, hh, hc, gg, gc, ph, phc, pg, pgc, sh, sg,
    send_sem, h1_sem, h2_sem, g1_sem, g2_sem, y_sem, own_sem,
):
    here = lax.axis_index("dp")
    y = lax.axis_index("expert")
    z, q = here // n, here % n
    twin = q + 1 - 2 * (q % 2)
    over = (q + n // 2) % n
    far = (twin + n // 2) % n
    zs = [(z + d) % n for d in range(n)]
    qs = [(q + d) % n for d in range(n)]

    barrier = pltpu.get_barrier_semaphore()
    peers = [(here, 1 - y)]
    peers += [(zs[d] * n + q, y) for d in range(1, n)]
    peers += [(z * n + qs[d], y) for d in range(1, n)]
    for peer in peers:
        pl.semaphore_signal(barrier, inc=1, device_id=peer, device_id_type=MESH)
    pl.semaphore_wait(barrier, len(peers))

    ends = []

    def send(src, dst, sem, peer, when=None):
        copy = pltpu.make_async_remote_copy(
            src_ref=src,
            dst_ref=dst,
            send_sem=send_sem.at[len(ends)],
            recv_sem=sem,
            device_id=peer,
            device_id_type=MESH,
        )
        ends.append((copy, when))
        if when is None:
            copy.start()
        else:
            pl.when(when)(copy.start)

    def landed(view, sem):
        pltpu.make_async_copy(view, view, sem).wait()

    h_at = lambda i, k, b: hh.at[i, k, b] if b < 2 else hc.at[i, k]
    g_at = lambda i, k, b: gg.at[i, k, b] if b < 2 else gc.at[i, k]
    h_all = lambda k, b: hh.at[:, k, b] if b < 2 else hc.at[:, k]
    g_all = lambda i, b: gg.at[i, :, b] if b < 2 else gc.at[i]
    h_from = lambda b, i: (h_o.at[0, i], ph.at[i], sh.at[i])[b]
    g_from = lambda b, i: (g_o.at[0, i], pg.at[i], sg.at[i])[b]

    def own_h(b):
        return pltpu.make_async_copy(h_from(b, z), h_at(z, q, b), own_sem.at[2 * b])

    def own_g(b):
        return pltpu.make_async_copy(g_from(b, q), g_at(z, q, b), own_sem.at[2 * b + 1])

    def start_g(b):
        for d in range(1, n):
            peer = (z * n + qs[d], y)
            send(g_from(b, qs[d]), g_at(z, q, b), g1_sem.at[b * n + q], peer)
        own_g(b).start()

    def start_h(b):
        for d in range(1, n):
            peer = (zs[d] * n + q, y)
            send(h_from(b, zs[d]), h_at(z, q, b), h1_sem.at[b * n + z], peer)
        own_h(b).start()

    def up_g(i, b, when):
        peer = (jnp.minimum(z + 1, n - 1) * n + q, y)
        send(g_all(i, b), g_all(i, b), g2_sem.at[b * n + i], peer, when)

    def down_g(i, b, when):
        peer = (jnp.maximum(z - 1, 0) * n + q, y)
        send(g_all(i, b), g_all(i, b), g2_sem.at[b * n + i], peer, when)

    def plane_g(b):
        own_g(b).wait()
        for d in range(1, n):
            landed(g_at(z, qs[d], b), g1_sem.at[b * n + qs[d]])
        up_g(z, b, z + 1 < n)
        down_g(z, b, z >= 1)

    def forward_g(b, d):
        low = jnp.maximum(z - d, 0)
        high = jnp.minimum(z + d, n - 1)

        @pl.when(z - d >= 0)
        def _():
            landed(g_all(low, b), g2_sem.at[b * n + low])

        if d < n - 1:
            up_g(low, b, jnp.logical_and(z + 1 < n, z - d >= 0))

        @pl.when(z + d < n)
        def _():
            landed(g_all(high, b), g2_sem.at[b * n + high])

        if d < n - 1:
            down_g(high, b, jnp.logical_and(z >= 1, z + d < n))

    def fan_h(b):
        own_h(b).wait()
        for d in range(1, n):
            landed(h_at(zs[d], q, b), h1_sem.at[b * n + zs[d]])
        for to in (over, twin):
            send(h_all(q, b), h_all(q, b), h2_sem.at[b * n + q], (z * n + to, y))

    def relay_h(b):
        landed(h_all(over, b), h2_sem.at[b * n + over])
        send(h_all(over, b), h_all(over, b), h2_sem.at[b * n + over], (z * n + twin, y))

    across = (here, 1 - y)
    start_g(0)
    start_h(0)
    send(g_o.at[1], pg, y_sem.at[0], across)
    send(h_o.at[1], ph, y_sem.at[1], across)
    send(g_c.at[1], pgc, y_sem.at[2], across)
    send(h_c.at[1], phc, y_sem.at[3], across)
    plane_g(0)
    fan_h(0)
    landed(pg, y_sem.at[0])
    start_g(1)
    forward_g(0, 1)
    landed(ph, y_sem.at[1])
    start_h(1)
    plane_g(1)
    forward_g(0, 2)
    relay_h(0)
    landed(pgc, y_sem.at[2])
    landed(phc, y_sem.at[3])
    sg[...] = g_c[0] + pgc[...]
    sh[...] = h_c[0] + phc[...]
    fan_h(1)
    start_g(2)
    start_h(2)
    forward_g(1, 1)
    plane_g(2)
    relay_h(1)
    fan_h(2)
    forward_g(1, 2)
    forward_g(2, 1)
    relay_h(2)
    forward_g(2, 2)
    for b in range(3):
        forward_g(b, n - 1)
        for k in (twin, far):
            landed(h_all(k, b), h2_sem.at[b * n + k])
    for copy, when in ends:
        if when is None:
            copy.wait_send()
        else:
            pl.when(when)(copy.wait_send)


def n_sends(n):
    return 4 + 3 * (2 * (n - 1) + 2 + 2 * (n - 2) + 3)


def gather_pairs(hidden, out_grad, counts, route_index, keep, capacity):
    replicas = lax.axis_size("dp")
    n = math.isqrt(replicas)
    hcols, gcols = hidden.shape[1] // n, out_grad.shape[1] // n
    big = capacity // SUB * SUB
    rest = capacity - big
    kind = jnp.bfloat16
    vmem = pl.BlockSpec(memory_space=pltpu.VMEM)
    smem = pl.BlockSpec(memory_space=pltpu.SMEM)
    made = pl.pallas_call(
        functools.partial(slots_kernel, n, big, rest),
        out_shape=[
            jax.ShapeDtypeStruct((2, n, big, hcols), kind),
            jax.ShapeDtypeStruct((2, n, 2 * rest, hcols), kind),
            jax.ShapeDtypeStruct((2, n, big, gcols), kind),
            jax.ShapeDtypeStruct((2, n, 2 * rest, gcols), kind),
        ],
        in_specs=[smem, smem, vmem, vmem, vmem],
        out_specs=[vmem] * 4,
        compiler_params=pltpu.CompilerParams(vmem_limit_bytes=16 << 20),
        name="slots",
    )(counts, keep, route_index, hidden, out_grad)
    hh, hc, gg, gc = pl.pallas_call(
        functools.partial(spread_kernel, n),
        out_shape=[
            jax.ShapeDtypeStruct((n, n, 2, big, hcols), kind),
            jax.ShapeDtypeStruct((n, n, 2 * rest, hcols), kind),
            jax.ShapeDtypeStruct((n, n, 2, big, gcols), kind),
            jax.ShapeDtypeStruct((n, n, 2 * rest, gcols), kind),
        ],
        in_specs=[vmem] * 4,
        out_specs=[vmem] * 4,
        scratch_shapes=[
            pltpu.VMEM((n, big, hcols), kind),
            pltpu.VMEM((n, 2 * rest, hcols), kind),
            pltpu.VMEM((n, big, gcols), kind),
            pltpu.VMEM((n, 2 * rest, gcols), kind),
            pltpu.VMEM((n, 2 * rest, hcols), kind),
            pltpu.VMEM((n, 2 * rest, gcols), kind),
            pltpu.SemaphoreType.DMA((n_sends(n),)),
            pltpu.SemaphoreType.DMA((3 * n,)),
            pltpu.SemaphoreType.DMA((3 * n,)),
            pltpu.SemaphoreType.DMA((3 * n,)),
            pltpu.SemaphoreType.DMA((3 * n,)),
            pltpu.SemaphoreType.DMA((4,)),
            pltpu.SemaphoreType.DMA((6,)),
        ],
        compiler_params=pltpu.CompilerParams(
            collective_id=0, has_side_effects=True, vmem_limit_bytes=24 << 20
        ),
        name="spread",
    )(*made)
    return [
        (hh.reshape(-1, hcols), gg.reshape(-1, gcols)),
        (hc.reshape(-1, hcols), gc.reshape(-1, gcols)),
    ]


def tile_kernel(pairs, keep, *refs):
    out, scales = refs[2 * pairs :]
    replicas = keep.shape[0]
    kept = keep[0]
    for i in range(1, replicas):
        kept = kept + keep[i]
    factor = jnp.float32(replicas) / jnp.maximum(
        jnp.full((1, LANES), kept, jnp.int32).astype(jnp.float32), 1.0
    )
    total = None
    for i in range(pairs):
        term = lax.dot_general(
            refs[2 * i][...],
            refs[2 * i + 1][...],
            (((0,), (0,)), ((), ())),
            preferred_element_type=jnp.float32,
        )
        total = term if total is None else total + term
    tops = []
    for b in range(out.shape[1] // LANES):
        block = total[:, b * LANES : (b + 1) * LANES] * factor
        top = jnp.max(jnp.abs(block), axis=1, keepdims=True)
        out[:, b * LANES : (b + 1) * LANES] = block * (1.0 / (top + 1e-6))
        tops.append(top)
    lane = lax.broadcasted_iota(jnp.int32, (out.shape[0], LANES), 1)
    packed = jnp.zeros((out.shape[0], LANES), jnp.float32)
    for b, top in enumerate(tops):
        packed = jnp.where(lane == b, top, packed)
    spun = packed.T
    for b in range(scales.shape[0]):
        scales[b] = spun[b : b + 1]


def tile_grad(pairs, keep):
    rows, cols = pairs[0][0].shape[1], pairs[0][1].shape[1]
    step = min(rows, 512)
    args, specs = [], []
    for h, g in pairs:
        args += [h, g]
        specs.append(pl.BlockSpec((h.shape[0], step), lambda i: (0, i)))
        specs.append(pl.BlockSpec((g.shape[0], cols), lambda i: (0, 0)))
    return pl.pallas_call(
        functools.partial(tile_kernel, len(pairs)),
        grid=(rows // step,),
        out_shape=[
            jax.ShapeDtypeStruct((rows, cols), jnp.float32),
            jax.ShapeDtypeStruct((cols // LANES, 1, rows), jnp.float32),
        ],
        in_specs=[pl.BlockSpec(memory_space=pltpu.SMEM)] + specs,
        out_specs=[
            pl.BlockSpec((step, cols), lambda i: (i, 0)),
            pl.BlockSpec((cols // LANES, 1, step), lambda i: (0, 0, i)),
        ],
        compiler_params=pltpu.CompilerParams(vmem_limit_bytes=32 << 20),
        name="tile_grad",
    )(keep, *args)


def on_device(hidden, out_grad, counts, route_index, keep):
    experts = lax.axis_size("expert")
    tok_rows = hidden.shape[0]
    capacity = max(tok_rows // 4, tok_rows // experts + 4)
    rest = capacity % SUB
    paired = experts == 2 and lax.axis_size("dp") == 16 and capacity == SUB + rest and 2 * rest == SUB // 2
    gather = gather_pairs if paired else gather_general
    pairs = gather(hidden, out_grad, counts, route_index, keep, capacity)
    normed, scales = tile_grad(pairs, keep)
    return (normed[None, None], jnp.transpose(scales[None], (0, 2, 3, 1)))


def solution(mesh):
    placed = (
        P(("dp", "expert"), None),
        P(("dp", "expert"), None),
        P(("dp", "expert"), None),
        P(("dp", "expert"), None),
        P(),
    )
    return jax.shard_map(
        on_device,
        mesh=mesh,
        in_specs=placed,
        out_specs=(P("expert", "dp", None, None), P("expert", "dp", None, None)),
        check_vma=False,
    )
```

```python
import functools
import math

import jax
import jax.numpy as jnp
from jax import lax
from jax.experimental import pallas as pl
from jax.experimental.pallas import tpu as pltpu
from jax.sharding import PartitionSpec as P

MESH = pl.DeviceIdType.MESH
LANES = 128
SUB = 16


def swapped(block, axis, bit):
    count = lax.axis_size(axis)
    route = []
    for low in range(count):
        high = low | 1 << bit
        if high != low and high < count:
            route += [(low, high), (high, low)]
    return lax.ppermute(block, axis, route)


def build_slots(rows_dev, counts_dev, perm_dev, capacity):
    offsets = jnp.cumsum(counts_dev) - counts_dev
    slots = jnp.arange(capacity, dtype=jnp.int32)
    position = offsets[:, None] + slots[None, :]
    position = jnp.minimum(position, rows_dev.shape[0] - 1)
    live = slots[None, :] < counts_dev[:, None]
    local = perm_dev[position]
    picked = rows_dev[local]
    return jnp.where(live[:, :, None], picked, jnp.zeros_like(picked))


def join_pair(mine, partner, replica, bit):
    lower = replica >> bit & 1 == 0
    first = jnp.concatenate([mine, partner], axis=1)
    second = jnp.concatenate([partner, mine], axis=1)
    return jnp.where(lower, first, second)


def gather_general(hidden, out_grad, counts, route_index, keep, capacity):
    experts = lax.axis_size("expert")
    replicas = lax.axis_size("dp")
    side = math.isqrt(replicas)
    levels = side.bit_length() - 1
    replica = lax.axis_index("dp")
    hidden_units = hidden.shape[1]
    width = out_grad.shape[1]
    grad_rows = jnp.where(keep[replica] > 0, out_grad, jnp.zeros_like(out_grad))
    send_h = build_slots(hidden, counts[0], route_index[0], capacity)
    send_g = build_slots(grad_rows, counts[0], route_index[0], capacity)
    recv_h = lax.all_to_all(send_h, "expert", split_axis=0, concat_axis=0, tiled=True)
    recv_g = lax.all_to_all(send_g, "expert", split_axis=0, concat_axis=0, tiled=True)
    slot_count = experts * capacity
    tile_rows = hidden_units // side
    tile_cols = width // side
    sub_rows = slot_count // side
    piece_h = (
        recv_h.reshape(side, sub_rows, side, tile_rows)
        .transpose(2, 0, 1, 3)
        .reshape(replicas, sub_rows, tile_rows)
    )
    piece_g = (
        recv_g.reshape(side, sub_rows, side, tile_cols)
        .transpose(0, 2, 1, 3)
        .reshape(replicas, sub_rows, tile_cols)
    )
    all_h = lax.all_to_all(piece_h, "dp", split_axis=0, concat_axis=0, tiled=True)
    all_g = lax.all_to_all(piece_g, "dp", split_axis=0, concat_axis=0, tiled=True)
    for bit in range(levels):
        all_h = join_pair(all_h, swapped(all_h, "dp", bit), replica, bit)
    for bit in range(levels, 2 * levels):
        all_g = join_pair(all_g, swapped(all_g, "dp", bit), replica, bit)
    return [(all_h.reshape(-1, tile_rows), all_g.reshape(-1, tile_cols))]


def slots_kernel(
    side, big, rest, counts_in, keep_in, route_in, hidden_in, grad_in, h_o, h_c, g_o, g_c,
    counts, keep, route, hidden, grad, sems,
):
    moves = []
    for src, dst in ((counts_in, counts), (keep_in, keep), (route_in, route)):
        moves.append(pltpu.make_async_copy(src, dst, sems.at[len(moves)]))
    for src, dst in ((hidden_in, hidden), (grad_in, grad)):
        cols = src.shape[1] // side
        for part in range(side):
            cut = (slice(None), pl.ds(part * cols, cols))
            move = pltpu.make_async_copy(src.at[cut], dst.at[cut], sems.at[len(moves)])
            moves.append(move)
    for move in moves:
        move.start()
    for move in moves[:3]:
        move.wait()
    due = moves[3:]
    me = lax.axis_index("expert")
    rows = hidden.shape[0]
    total = 2 * big + 4 * rest
    row = lax.broadcasted_iota(jnp.int32, (total, rows), 0)
    pos = lax.broadcasted_iota(jnp.int32, (total, rows), 1)
    tail = row >= 2 * big
    in_tail = row - 2 * big
    other = jnp.logical_or(
        in_tail >= 2 * rest, jnp.logical_and(row >= big, jnp.logical_not(tail))
    )
    tail_row = jnp.where(in_tail >= 2 * rest, in_tail - 2 * rest, in_tail) - me * rest
    slot = jnp.where(tail, big + tail_row, jnp.where(row >= big, row - big, row))
    valid = jnp.logical_or(
        jnp.logical_not(tail), jnp.logical_and(tail_row >= 0, tail_row < rest)
    )
    first, second = counts[0, 0], counts[0, 1]
    expert = jnp.where(other, 1 - me, me)
    start = jnp.where(expert == 0, 0, first)
    count = jnp.where(expert == 0, first, second)
    take = jnp.logical_and(valid, jnp.logical_and(slot < count, pos == start + slot))
    take = jnp.where(take, 1.0, 0.0).astype(jnp.bfloat16)
    local = lax.broadcasted_iota(jnp.int32, (rows, rows), 0)
    perm = jnp.where(local == route[...], 1.0, 0.0).astype(jnp.bfloat16)
    pick = lax.dot_general(
        take, perm, (((1,), (1,)), ((), ())), preferred_element_type=jnp.float32
    )
    kept = keep[lax.axis_index("dp")] > 0
    pick_h = pick.astype(jnp.bfloat16)
    pick_g = jnp.where(kept, pick, 0.0).astype(jnp.bfloat16)
    for pick_x, src, o_ref, c_ref in ((pick_h, hidden, h_o, h_c), (pick_g, grad, g_o, g_c)):
        cols = o_ref.shape[3]
        for part in range(side):
            due.pop(0).wait()
            got = jnp.dot(
                pick_x,
                src[:, part * cols : (part + 1) * cols],
                preferred_element_type=jnp.float32,
            ).astype(jnp.bfloat16)
            for k in range(2):
                o_ref[k, part] = got[k * big : (k + 1) * big]
                low = 2 * big + 2 * rest * k
                c_ref[k, part] = got[low : low + 2 * rest]


def spread_kernel(
    n, h_o, h_c, g_o, g_c, hh, hc, gg, gc, ph, phc, pg, pgc, sh, sg,
    send_sem, h1_sem, h2_sem, g1_sem, g2_sem, y_sem, own_sem,
):
    here = lax.axis_index("dp")
    y = lax.axis_index("expert")
    z, q = here // n, here % n
    twin = q + 1 - 2 * (q % 2)
    over = (q + n // 2) % n
    far = (twin + n // 2) % n
    zs = [(z + d) % n for d in range(n)]
    qs = [(q + d) % n for d in range(n)]

    barrier = pltpu.get_barrier_semaphore()
    peers = [(here, 1 - y)]
    peers += [(zs[d] * n + q, y) for d in range(1, n)]
    peers += [(z * n + qs[d], y) for d in range(1, n)]
    for peer in peers:
        pl.semaphore_signal(barrier, inc=1, device_id=peer, device_id_type=MESH)
    pl.semaphore_wait(barrier, len(peers))

    ends = []

    def send(src, dst, sem, peer, when=None):
        copy = pltpu.make_async_remote_copy(
            src_ref=src,
            dst_ref=dst,
            send_sem=send_sem.at[len(ends)],
            recv_sem=sem,
            device_id=peer,
            device_id_type=MESH,
        )
        ends.append((copy, when))
        if when is None:
            copy.start()
        else:
            pl.when(when)(copy.start)

    def landed(view, sem):
        pltpu.make_async_copy(view, view, sem).wait()

    h_at = lambda i, k, b: hh.at[i, k, b] if b < 2 else hc.at[i, k]
    g_at = lambda i, k, b: gg.at[i, k, b] if b < 2 else gc.at[i, k]
    h_all = lambda k, b: hh.at[:, k, b] if b < 2 else hc.at[:, k]
    g_all = lambda i, b: gg.at[i, :, b] if b < 2 else gc.at[i]
    h_from = lambda b, i: (h_o.at[0, i], ph.at[i], sh.at[i])[b]
    g_from = lambda b, i: (g_o.at[0, i], pg.at[i], sg.at[i])[b]

    def own_h(b):
        return pltpu.make_async_copy(h_from(b, z), h_at(z, q, b), own_sem.at[2 * b])

    def own_g(b):
        return pltpu.make_async_copy(g_from(b, q), g_at(z, q, b), own_sem.at[2 * b + 1])

    def start_g(b):
        for d in range(1, n):
            peer = (z * n + qs[d], y)
            send(g_from(b, qs[d]), g_at(z, q, b), g1_sem.at[b * n + q], peer)
        own_g(b).start()

    def start_h(b):
        for d in range(1, n):
            peer = (zs[d] * n + q, y)
            send(h_from(b, zs[d]), h_at(z, q, b), h1_sem.at[b * n + z], peer)
        own_h(b).start()

    def up_g(i, b, when):
        peer = (jnp.minimum(z + 1, n - 1) * n + q, y)
        send(g_all(i, b), g_all(i, b), g2_sem.at[b * n + i], peer, when)

    def down_g(i, b, when):
        peer = (jnp.maximum(z - 1, 0) * n + q, y)
        send(g_all(i, b), g_all(i, b), g2_sem.at[b * n + i], peer, when)

    def plane_g(b):
        own_g(b).wait()
        for d in range(1, n):
            landed(g_at(z, qs[d], b), g1_sem.at[b * n + qs[d]])
        up_g(z, b, z + 1 < n)
        down_g(z, b, z >= 1)

    def forward_g(b, d):
        low = jnp.maximum(z - d, 0)
        high = jnp.minimum(z + d, n - 1)

        @pl.when(z - d >= 0)
        def _():
            landed(g_all(low, b), g2_sem.at[b * n + low])

        if d < n - 1:
            up_g(low, b, jnp.logical_and(z + 1 < n, z - d >= 0))

        @pl.when(z + d < n)
        def _():
            landed(g_all(high, b), g2_sem.at[b * n + high])

        if d < n - 1:
            down_g(high, b, jnp.logical_and(z >= 1, z + d < n))

    def fan_h(b):
        own_h(b).wait()
        for d in range(1, n):
            landed(h_at(zs[d], q, b), h1_sem.at[b * n + zs[d]])
        for to in (over, twin):
            send(h_all(q, b), h_all(q, b), h2_sem.at[b * n + q], (z * n + to, y))

    def relay_h(b):
        landed(h_all(over, b), h2_sem.at[b * n + over])
        send(h_all(over, b), h_all(over, b), h2_sem.at[b * n + over], (z * n + twin, y))

    across = (here, 1 - y)
    start_g(0)
    start_h(0)
    send(g_o.at[1], pg, y_sem.at[0], across)
    send(h_o.at[1], ph, y_sem.at[1], across)
    send(g_c.at[1], pgc, y_sem.at[2], across)
    send(h_c.at[1], phc, y_sem.at[3], across)
    plane_g(0)
    fan_h(0)
    landed(pg, y_sem.at[0])
    start_g(1)
    forward_g(0, 1)
    landed(ph, y_sem.at[1])
    start_h(1)
    plane_g(1)
    forward_g(0, 2)
    relay_h(0)
    landed(pgc, y_sem.at[2])
    landed(phc, y_sem.at[3])
    sg[...] = g_c[0] + pgc[...]
    sh[...] = h_c[0] + phc[...]
    fan_h(1)
    start_g(2)
    start_h(2)
    forward_g(1, 1)
    plane_g(2)
    relay_h(1)
    fan_h(2)
    forward_g(1, 2)
    forward_g(2, 1)
    relay_h(2)
    forward_g(2, 2)
    for b in range(3):
        forward_g(b, n - 1)
        for k in (twin, far):
            landed(h_all(k, b), h2_sem.at[b * n + k])
    for copy, when in ends:
        if when is None:
            copy.wait_send()
        else:
            pl.when(when)(copy.wait_send)


def n_sends(n):
    return 4 + 3 * (2 * (n - 1) + 2 + 2 * (n - 2) + 3)


def gather_pairs(hidden, out_grad, counts, route_index, keep, capacity):
    replicas = lax.axis_size("dp")
    n = math.isqrt(replicas)
    hcols, gcols = hidden.shape[1] // n, out_grad.shape[1] // n
    big = capacity // SUB * SUB
    rest = capacity - big
    kind = jnp.bfloat16
    vmem = pl.BlockSpec(memory_space=pltpu.VMEM)
    made = pl.pallas_call(
        functools.partial(slots_kernel, n, big, rest),
        out_shape=[
            jax.ShapeDtypeStruct((2, n, big, hcols), kind),
            jax.ShapeDtypeStruct((2, n, 2 * rest, hcols), kind),
            jax.ShapeDtypeStruct((2, n, big, gcols), kind),
            jax.ShapeDtypeStruct((2, n, 2 * rest, gcols), kind),
        ],
        in_specs=[pl.BlockSpec(memory_space=pltpu.HBM)] * 5,
        out_specs=[vmem] * 4,
        scratch_shapes=[
            pltpu.SMEM(counts.shape, counts.dtype),
            pltpu.SMEM(keep.shape, keep.dtype),
            pltpu.VMEM(route_index.shape, route_index.dtype),
            pltpu.VMEM(hidden.shape, kind),
            pltpu.VMEM(out_grad.shape, kind),
            pltpu.SemaphoreType.DMA((3 + 2 * n,)),
        ],
        compiler_params=pltpu.CompilerParams(vmem_limit_bytes=16 << 20),
        name="slots",
    )(*[pltpu.with_memory_space_constraint(x, pltpu.HBM) for x in (counts, keep, route_index, hidden, out_grad)])
    hh, hc, gg, gc = pl.pallas_call(
        functools.partial(spread_kernel, n),
        out_shape=[
            jax.ShapeDtypeStruct((n, n, 2, big, hcols), kind),
            jax.ShapeDtypeStruct((n, n, 2 * rest, hcols), kind),
            jax.ShapeDtypeStruct((n, n, 2, big, gcols), kind),
            jax.ShapeDtypeStruct((n, n, 2 * rest, gcols), kind),
        ],
        in_specs=[vmem] * 4,
        out_specs=[vmem] * 4,
        scratch_shapes=[
            pltpu.VMEM((n, big, hcols), kind),
            pltpu.VMEM((n, 2 * rest, hcols), kind),
            pltpu.VMEM((n, big, gcols), kind),
            pltpu.VMEM((n, 2 * rest, gcols), kind),
            pltpu.VMEM((n, 2 * rest, hcols), kind),
            pltpu.VMEM((n, 2 * rest, gcols), kind),
            pltpu.SemaphoreType.DMA((n_sends(n),)),
            pltpu.SemaphoreType.DMA((3 * n,)),
            pltpu.SemaphoreType.DMA((3 * n,)),
            pltpu.SemaphoreType.DMA((3 * n,)),
            pltpu.SemaphoreType.DMA((3 * n,)),
            pltpu.SemaphoreType.DMA((4,)),
            pltpu.SemaphoreType.DMA((6,)),
        ],
        compiler_params=pltpu.CompilerParams(
            collective_id=0, has_side_effects=True, vmem_limit_bytes=24 << 20
        ),
        name="spread",
    )(*made)
    return [
        (hh.reshape(-1, hcols), gg.reshape(-1, gcols)),
        (hc.reshape(-1, hcols), gc.reshape(-1, gcols)),
    ]


def tile_kernel(pairs, keep, *refs):
    out, scales = refs[2 * pairs :]
    replicas = keep.shape[0]
    kept = keep[0]
    for i in range(1, replicas):
        kept = kept + keep[i]
    factor = jnp.float32(replicas) / jnp.maximum(
        jnp.full((1, LANES), kept, jnp.int32).astype(jnp.float32), 1.0
    )
    total = None
    for i in range(pairs):
        term = lax.dot_general(
            refs[2 * i][...],
            refs[2 * i + 1][...],
            (((0,), (0,)), ((), ())),
            preferred_element_type=jnp.float32,
        )
        total = term if total is None else total + term
    tops = []
    for b in range(out.shape[1] // LANES):
        block = total[:, b * LANES : (b + 1) * LANES] * factor
        top = jnp.max(jnp.abs(block), axis=1, keepdims=True)
        out[:, b * LANES : (b + 1) * LANES] = block * (1.0 / (top + 1e-6))
        tops.append(top)
    lane = lax.broadcasted_iota(jnp.int32, (out.shape[0], LANES), 1)
    packed = jnp.zeros((out.shape[0], LANES), jnp.float32)
    for b, top in enumerate(tops):
        packed = jnp.where(lane == b, top, packed)
    spun = packed.T
    for b in range(scales.shape[0]):
        scales[b] = spun[b : b + 1]


def tile_grad(pairs, keep):
    rows, cols = pairs[0][0].shape[1], pairs[0][1].shape[1]
    step = min(rows, 512)
    args, specs = [], []
    for h, g in pairs:
        args += [h, g]
        specs.append(pl.BlockSpec((h.shape[0], step), lambda i: (0, i)))
        specs.append(pl.BlockSpec((g.shape[0], cols), lambda i: (0, 0)))
    return pl.pallas_call(
        functools.partial(tile_kernel, len(pairs)),
        grid=(rows // step,),
        out_shape=[
            jax.ShapeDtypeStruct((rows, cols), jnp.float32),
            jax.ShapeDtypeStruct((cols // LANES, 1, rows), jnp.float32),
        ],
        in_specs=[pl.BlockSpec(memory_space=pltpu.SMEM)] + specs,
        out_specs=[
            pl.BlockSpec((step, cols), lambda i: (i, 0)),
            pl.BlockSpec((cols // LANES, 1, step), lambda i: (0, 0, i)),
        ],
        compiler_params=pltpu.CompilerParams(vmem_limit_bytes=32 << 20),
        name="tile_grad",
    )(keep, *args)


def on_device(hidden, out_grad, counts, route_index, keep):
    experts = lax.axis_size("expert")
    tok_rows = hidden.shape[0]
    capacity = max(tok_rows // 4, tok_rows // experts + 4)
    rest = capacity % SUB
    paired = experts == 2 and lax.axis_size("dp") == 16 and capacity == SUB + rest and 2 * rest == SUB // 2
    gather = gather_pairs if paired else gather_general
    pairs = gather(hidden, out_grad, counts, route_index, keep, capacity)
    normed, scales = tile_grad(pairs, keep)
    return (normed[None, None], jnp.transpose(scales[None], (0, 2, 3, 1)))


def solution(mesh):
    placed = (
        P(("dp", "expert"), None),
        P(("dp", "expert"), None),
        P(("dp", "expert"), None),
        P(("dp", "expert"), None),
        P(),
    )
    return jax.shard_map(
        on_device,
        mesh=mesh,
        in_specs=placed,
        out_specs=(P("expert", "dp", None, None), P("expert", "dp", None, None)),
        check_vma=False,
    )
```
